32 devices in a mesh: cols: 8 (over z, y), chan: 4 (over x, core).
Axes of the slice: x: 2, y: 2, z: 4, core: 2. Of those that a mesh axis runs over, the one named last changes fastest.
Arguments:
- anomaly: bfloat16 [2048, 80, 128], P('cols'), may hold values from -6 to 6
- jacobian: bfloat16 [1024, 256, 128], P(('cols', 'chan')), may hold values from -0.5 to 0.5
- foot_cols: int32 [1024, 4], P('cols'), may hold values from 0 to 2047, as said below
- foot_weight: float32 [1024, 4], P('cols'), may hold values from 0.1 to 1
- obs_count: int32 [8], P('cols'), may hold values from 32 to 128, as said below
- obs_weight: bfloat16 [256, 1024], P(None, ('cols', 'chan')), may hold values from 0.25 to 4
Outputs:
- radiance_pert: bfloat16 [80, 256, 1024], P(None, 'chan', 'cols')
- ensemble_gram: float32 [64, 80, 80], P('cols', 'chan')
The draws below stay inside these ranges and needn't reach their ends.
Inputs may be any that keep to these rules, and one draw needn't show every extreme that they name: `foot_cols`: the footprint columns of an observation of tile t lie among the columns t * 256 - 32 to (t + 1) * 256 + 31, taken modulo 2048. The live observations of tile t are its first obs_count[t] slots; in every draw at least one tile has all 128 slots live.
All inputs are finite; a program needn't handle non-finite values.
Results may differ from the reference program's by a relative error of at most 0.0095.
Values may be sent and summed in bfloat16 or wider, within the bound.
A program may use at most 64 MiB of HBM per device.

```python
import math
from functools import partial
import jax
import jax.numpy as jnp
from jax import lax

M = 80
LEV = 128
CH = 256
TCOL = 256
OBS_DEV = 128
FP = 4
HALO = 32
PTS = 8
NCOLS = 2048
NOBS = 1024


def draw_foot_cols(key, part):
    tile_index = (jnp.arange(NOBS, dtype=jnp.int32) // OBS_DEV)[:, None]
    base_offset = jax.random.randint(jax.random.fold_in(key, 11), (NOBS, 1), -HALO, TCOL + HALO - 5, dtype=jnp.int32)
    spread_offset = jax.random.randint(jax.random.fold_in(key, 12), (NOBS, FP), 0, 6, dtype=jnp.int32)
    return jnp.mod(tile_index * TCOL + base_offset + spread_offset, NCOLS).astype(jnp.int32)


def draw_obs_count(key, part):
    tile_count = NOBS // OBS_DEV
    counts = jax.random.randint(jax.random.fold_in(key, 21), (tile_count,), OBS_DEV // 4, OBS_DEV + 1, dtype=jnp.int32)
    full_tile = jax.random.randint(jax.random.fold_in(key, 22), (), 0, tile_count, dtype=jnp.int32)
    return jnp.where(jnp.arange(tile_count, dtype=jnp.int32) == full_tile, OBS_DEV, counts).astype(jnp.int32)


def shard_levels(own_key, dims, split, least, largest):
    gain = 1.0
    for position, shards_of in split:
        steps = jax.random.uniform(jax.random.fold_in(jax.random.fold_in(own_key, 6), position), (shards_of,), jnp.float32, least / len(split), largest / len(split))
        gain = gain * jnp.repeat(jnp.exp(steps), dims[position] // shards_of).reshape((-1,) + (1,) * (len(dims) - 1 - position))
    return gain


def noise(rng, dims, deviation, most, split=(), kind=jnp.bfloat16):
    gain = shard_levels(rng, dims, split, -0.22, 0.18) if split else 1.0
    entries = jax.random.normal(rng, dims, jnp.float32) * deviation * gain
    return jnp.minimum(jnp.maximum(entries, -most), most).astype(kind)


def setup_inputs(seed: int = 0) -> dict:
    streams_of = jax.random.split(jax.random.key(seed), 7)
    return {
        "anomaly": noise(streams_of[0], (NCOLS, M, LEV), 1.0, 6.0, ((0, 8),)),
        "jacobian": noise(streams_of[1], (NOBS, CH, LEV), LEV ** -0.5, 0.5, ((0, 32),)),
        "foot_cols": draw_foot_cols(jax.random.fold_in(streams_of[6], 71), 0),
        "foot_weight": jnp.clip(jnp.exp(math.log(1.0) - 2.3025851 * jax.random.uniform(streams_of[3], (NOBS, FP), jnp.float32) ** shard_levels(streams_of[3], (NOBS, FP), ((0, 8),), -0.2, 0.2)), 0.1, 1.0),
        "obs_count": draw_obs_count(jax.random.fold_in(streams_of[6], 71), 0),
        "obs_weight": jnp.clip(jnp.exp(math.log(4.0) - 2.7725887 * jax.random.uniform(streams_of[5], (CH, NOBS), jnp.float32) ** shard_levels(streams_of[5], (CH, NOBS), ((1, 32),), -0.2, 0.2)), 0.25, 4.0).astype(jnp.bfloat16),
    }


def taper(distance, half_width):
    relative = jnp.abs(distance) / half_width
    near_part = ((((-0.25 * relative + 0.5) * relative + 0.625) * relative - 5.0 / 3.0) * relative * relative) + 1.0
    bounded = jnp.maximum(relative, 1.0)
    far_part = (((((relative / 12.0 - 0.5) * relative + 0.625) * relative + 5.0 / 3.0) * relative - 5.0) * relative + 4.0) - 2.0 / (3.0 * bounded)
    return jnp.where(relative <= 1.0, near_part, jnp.where(relative <= 2.0, far_part, 0.0))


def local_gram(perturbed, error_weight, centers):
    spacing = TCOL / PTS
    points = (jnp.arange(PTS, dtype=jnp.float32) + 0.5) * spacing
    locality = taper(centers[None, :] - points[:, None], spacing)
    values = perturbed.astype(jnp.float32)
    weighted = values * error_weight.astype(jnp.float32)
    flat_values = values.reshape(values.shape[0], -1)
    gram_list = []
    for point_index in range(PTS):
        scaled = (weighted * locality[point_index][None, None, :]).astype(jnp.bfloat16)
        scaled = lax.optimization_barrier(scaled)
        flat_scaled = scaled.astype(jnp.float32).reshape(values.shape[0], -1)
        gram_list.append(jnp.dot(flat_scaled, flat_values.T, preferred_element_type=jnp.float32))
    return jnp.stack(gram_list) / (CH * OBS_DEV)


def tile_work(anomaly, inputs):
    tile_index, jacobian_tile, foot_tile, foot_gain, live_count, error_weight = inputs
    mixed_cols = jnp.zeros((OBS_DEV, M, LEV), jnp.float32)
    for column_slot in range(FP):
        mixed_cols = mixed_cols + foot_gain[:, column_slot, None, None] * anomaly[foot_tile[:, column_slot]].astype(jnp.float32)
    mixed_cols = lax.optimization_barrier(mixed_cols.astype(jnp.bfloat16))
    radiance = jnp.einsum("ncl,nml->mcn", jacobian_tile.astype(jnp.float32), mixed_cols.astype(jnp.float32))
    live_mask = (jnp.arange(OBS_DEV, dtype=jnp.int32) < live_count).astype(jnp.float32)
    perturbed = (radiance * live_mask[None, None, :]).astype(jnp.bfloat16)
    offsets = jnp.mod(foot_tile - tile_index * TCOL + HALO, NCOLS) - HALO
    centers = jnp.sum(foot_gain * offsets.astype(jnp.float32), axis=1) / jnp.sum(foot_gain, axis=1)
    return perturbed, local_gram(perturbed, error_weight[None], centers)


def reference(anomaly, jacobian, foot_cols, foot_weight, obs_count, obs_weight):
    tile_count = NOBS // OBS_DEV
    per_tile = (
        jnp.arange(tile_count, dtype=jnp.int32),
        jacobian.reshape(tile_count, OBS_DEV, CH, LEV),
        foot_cols.reshape(tile_count, OBS_DEV, FP),
        foot_weight.reshape(tile_count, OBS_DEV, FP),
        obs_count,
        obs_weight.reshape(CH, tile_count, OBS_DEV).transpose(1, 0, 2),
    )
    perturbed, gram_blocks = lax.map(partial(tile_work, anomaly), per_tile)
    radiance_pert = perturbed.transpose(1, 2, 0, 3).reshape(M, CH, NOBS)
    return radiance_pert, gram_blocks.reshape(tile_count * PTS, M, M)
```

```python
import functools

import jax
import jax.numpy as jnp
from jax import lax
from jax.experimental import pallas as pl
from jax.experimental.pallas import tpu as pltpu
from jax.sharding import PartitionSpec as P

HALO = 32
PTS = 8
LANES = 128
ROWS = 16
MESH = pl.DeviceIdType.MESH


def taper(distance, half_width):
    relative = jnp.abs(distance) / half_width
    near_part = (
        ((-0.25 * relative + 0.5) * relative + 0.625) * relative - 5.0 / 3.0
    ) * relative * relative + 1.0
    bounded = jnp.maximum(relative, 1.0)
    far_part = (
        ((((relative / 12.0 - 0.5) * relative + 0.625) * relative + 5.0 / 3.0) * relative - 5.0)
        * relative
        + 4.0
        - 2.0 / (3.0 * bounded)
    )
    return jnp.where(relative <= 1.0, near_part, jnp.where(relative <= 2.0, far_part, 0.0))


def kernel(
    ncols, nchan, anom, jac, fc_s, fw_s, cnt_s, fc_v, fw_v, ow_v, rad, gram, *scratch
):
    members = anom.shape[1]
    tile = anom.shape[0]
    obs, chans = jac.shape[0], jac.shape[1]
    slots = obs * nchan
    width = chans // nchan
    packs = LANES // width
    group = ROWS // packs
    chunks = members // ROWS
    rows = members // nchan
    foot = fc_v.shape[0]
    total = tile * ncols
    ext = scratch[:chunks]
    (jbuf, stage, sbuf, rbuf, rstore, wf, cent, loc, gs, gacc, gsend, grecv,
     sem_loc, sem_jac, sem_hs, sem_hr, sem_fs, sem_fr, sem_ss, sem_rs, sem_own,
     sem_gs, sem_gr) = scratch[chunks:]

    col = lax.axis_index("cols")
    chan = lax.axis_index("chan")
    core = lax.rem(chan, 2)
    partner = chan + 1 - 2 * core
    step = 1 - 2 * core
    ahead = lax.rem(col + step + ncols, ncols)
    behind = lax.rem(col - step + ncols, ncols)
    first = chan * obs

    barrier = pltpu.get_barrier_semaphore()
    for where in (ahead, behind):
        pl.semaphore_signal(barrier, inc=1, device_id=(where, chan), device_id_type=MESH)
    for d in range(1, nchan):
        pl.semaphore_signal(
            barrier, inc=1, device_id=(col, lax.rem(chan + d, nchan)), device_id_type=MESH
        )

    locals_ = []
    for k in range(chunks):
        copy = pltpu.make_async_copy(
            anom.at[:, pl.ds(k * ROWS, ROWS), :], ext[k].at[pl.ds(HALO, tile)], sem_loc.at[k]
        )
        copy.start()
        locals_.append(copy)
        if k == 0:
            jcopy = pltpu.make_async_copy(jac, jbuf, sem_jac.at[0])
            jcopy.start()

    pl.semaphore_wait(barrier, nchan + 1)
    src_col = (tile - HALO) * (1 - core)
    dst_col = (tile + HALO) * core
    halos = []
    for k in range(chunks):
        copy = pltpu.make_async_remote_copy(
            src_ref=anom.at[pl.ds(src_col, HALO), pl.ds(k * ROWS, ROWS), :],
            dst_ref=ext[k].at[pl.ds(dst_col, HALO)],
            send_sem=sem_hs.at[k],
            recv_sem=sem_hr.at[k],
            device_id=(ahead, chan),
            device_id_type=MESH,
        )
        copy.start()
        halos.append(copy)

    def offset_of(value):
        value = value - col * tile + HALO
        value = jnp.where(value < 0, value + total, value)
        return jnp.where(value >= total, value - total, value)

    gains = fw_v[...]
    offsets = (offset_of(fc_v[...]) - HALO).astype(jnp.float32)
    center = jnp.sum(gains * offsets, axis=0, keepdims=True) / jnp.sum(
        gains, axis=0, keepdims=True
    )
    cent[...] = jnp.transpose(jnp.broadcast_to(center, (LANES, slots)))
    mine = cent[pl.ds(pl.multiple_of(first, 8), obs), :]
    spacing = tile / PTS
    for p in range(PTS):
        loc[p] = taper(mine - (p + 0.5) * spacing, spacing) * (1.0 / (chans * slots))
    wf[...] = ow_v[...].astype(jnp.float32)

    lane = lax.broadcasted_iota(jnp.int32, (group, LANES), 1)
    live_count = cnt_s[0]
    jcopy.wait()

    sends = []
    for k in range(chunks):
        locals_[k].wait()
        halos[k].wait_recv()
        forward = pltpu.make_async_remote_copy(
            src_ref=ext[k].at[pl.ds(dst_col, HALO)],
            dst_ref=ext[k].at[pl.ds(dst_col, HALO)],
            send_sem=sem_fs.at[k],
            recv_sem=sem_fr.at[k],
            device_id=(col, partner),
            device_id_type=MESH,
        )
        forward.start()
        forward.wait_recv()

        def one(n, carry, k=k):
            slot = first + n
            mixed = None
            for f in range(foot):
                at = jnp.minimum(offset_of(fc_s[f, slot]), tile + 2 * HALO - 1)
                at = jnp.maximum(at, 0)
                part = fw_s[f, slot] * ext[k][at].astype(jnp.float32)
                mixed = part if mixed is None else mixed + part
            live = jnp.where(slot < live_count, 1.0, 0.0).astype(jnp.float32)
            radiance = lax.dot_general(
                mixed.astype(jnp.bfloat16), jbuf[n], (((1,), (1,)), ((), ())),
                preferred_element_type=jnp.float32,
            ) * live
            rstore[n, k * ROWS:(k + 1) * ROWS, :] = radiance.astype(jnp.bfloat16)
            for q in range(nchan):
                start = q * width
                block, shift = start // LANES * LANES, start % LANES
                piece = None
                for h in range(packs):
                    part = radiance[h * group:(h + 1) * group, block:block + LANES]
                    turn = (h * width - shift) % LANES
                    if turn:
                        part = pltpu.roll(part, turn, 1)
                    piece = part if piece is None else jnp.where(lane < h * width, piece, part)
                stage[q, pl.ds(n, group, stride=obs), :] = piece
            return carry

        lax.fori_loop(0, obs, one, 0, unroll=4)
        for q in range(nchan):
            sbuf[k, q] = stage[q].astype(jnp.bfloat16).reshape(group, obs, LANES)
        place = pl.ds(pl.multiple_of(first, obs), obs)
        for d in range(1, nchan):
            to = lax.rem(chan + d, nchan)
            copy = pltpu.make_async_remote_copy(
                src_ref=sbuf.at[k, to],
                dst_ref=rbuf.at[k, :, place, :],
                send_sem=sem_ss.at[k, d],
                recv_sem=sem_rs.at[k, d],
                device_id=(col, to),
                device_id_type=MESH,
            )
            copy.start()
            sends.append((k, copy))
        own = pltpu.make_async_copy(sbuf.at[k, chan], rbuf.at[k, :, place, :], sem_own.at[k])
        own.start()
        sends.append((k, own))
        forward.wait_send()
        halos[k].wait_send()

    def product(n, carry):
        values = rstore[n]
        weighted = (values.astype(jnp.float32) * wf[pl.ds(n, 1), :]).astype(jnp.bfloat16)
        gs[n] = lax.dot_general(
            weighted, values, (((1,), (1,)), ((), ())), preferred_element_type=jnp.float32
        )
        return carry

    lax.fori_loop(0, obs, product, 0, unroll=4)

    def point(p, carry):
        sums = [None, None]
        for n in range(obs):
            value = gs[n]
            for i in range(2):
                part = loc[2 * p + i, pl.ds(n, 1), :][:, :members] * value
                sums[i] = part if sums[i] is None else sums[i] + part
        for i in range(2):
            gacc[2 * p + i] = sums[i]
        return carry

    lax.fori_loop(0, PTS // 2, point, 0)
    for q in range(nchan):
        gsend[q] = gacc[:, q * rows:(q + 1) * rows, :].astype(jnp.bfloat16)
    gsends = []
    for d in range(1, nchan):
        to = lax.rem(chan + d, nchan)
        copy = pltpu.make_async_remote_copy(
            src_ref=gsend.at[to],
            dst_ref=grecv.at[d],
            send_sem=sem_gs.at[d],
            recv_sem=sem_gr.at[d],
            device_id=(col, to),
            device_id_type=MESH,
        )
        copy.start()
        gsends.append(copy)

    for k in range(chunks):
        for at, copy in sends:
            if at == k:
                copy.wait()

        def turn_one(j, carry, k=k):
            turned = jnp.transpose(rbuf[k, j].astype(jnp.float32)).astype(jnp.bfloat16)
            for h in range(packs):
                rad[k * ROWS + h * group + j] = turned[h * width:(h + 1) * width]
            return carry

        lax.fori_loop(0, group, turn_one, 0, unroll=2)

    result = gsend[chan].astype(jnp.float32)
    for d in range(1, nchan):
        gsends[d - 1].wait()
        result = result + grecv[d].astype(jnp.float32)
    gram[...] = result


def shards(ncols, nchan, anomaly, jacobian, foot_cols, foot_weight, obs_count, obs_weight):
    tile, members, levels = anomaly.shape
    obs, chans = jacobian.shape[:2]
    slots, foot = foot_cols.shape
    width = chans // nchan
    group = ROWS // (LANES // width)
    chunks = members // ROWS
    rows = members // nchan
    cols_t, gains_t = foot_cols.T, foot_weight.T
    vmem = pl.BlockSpec(memory_space=pltpu.VMEM)
    smem = pl.BlockSpec(memory_space=pltpu.SMEM)
    anyspace = pl.BlockSpec(memory_space=pl.ANY)
    dma = pltpu.SemaphoreType.DMA
    return pl.pallas_call(
        functools.partial(kernel, ncols, nchan),
        out_shape=(
            jax.ShapeDtypeStruct((members, width, slots), jnp.bfloat16),
            jax.ShapeDtypeStruct((PTS, rows, members), jnp.float32),
        ),
        in_specs=[anyspace, anyspace, smem, smem, smem, vmem, vmem, vmem],
        out_specs=(vmem, vmem),
        scratch_shapes=[
            *[pltpu.VMEM((tile + 2 * HALO, ROWS, levels), jnp.bfloat16) for _ in range(chunks)],
            pltpu.VMEM((obs, chans, levels), jnp.bfloat16),
            pltpu.VMEM((nchan, group * obs, LANES), jnp.float32),
            pltpu.VMEM((chunks, nchan, group, obs, LANES), jnp.bfloat16),
            pltpu.VMEM((chunks, group, slots, LANES), jnp.bfloat16),
            pltpu.VMEM((obs, members, chans), jnp.bfloat16),
            pltpu.VMEM((obs, chans), jnp.float32),
            pltpu.VMEM((slots, LANES), jnp.float32),
            pltpu.VMEM((PTS, obs, LANES), jnp.float32),
            pltpu.VMEM((obs, members, members), jnp.float32),
            pltpu.VMEM((PTS, members, members), jnp.float32),
            pltpu.VMEM((nchan, PTS, rows, members), jnp.bfloat16),
            pltpu.VMEM((nchan, PTS, rows, members), jnp.bfloat16),
            dma((chunks,)),
            dma((1,)),
            dma((chunks,)),
            dma((chunks,)),
            dma((chunks,)),
            dma((chunks,)),
            dma((chunks, nchan)),
            dma((chunks, nchan)),
            dma((chunks,)),
            dma((nchan,)),
            dma((nchan,)),
        ],
        compiler_params=pltpu.CompilerParams(
            collective_id=0, has_side_effects=True, vmem_limit_bytes=48 * 1024 * 1024
        ),
    )(anomaly, jacobian, cols_t, gains_t, obs_count, cols_t, gains_t, obs_weight.T)


def solution(mesh):
    return jax.shard_map(
        functools.partial(shards, mesh.shape["cols"], mesh.shape["chan"]),
        mesh=mesh,
        in_specs=(
            P("cols", None, None),
            P(("cols", "chan"), None, None),
            P("cols", None),
            P("cols", None),
            P("cols"),
            P(None, ("cols", "chan")),
        ),
        out_specs=(P(None, "chan", "cols"), P("cols", "chan", None)),
        check_vma=False,
    )
```

```python
import functools

import jax
import jax.numpy as jnp
from jax import lax
from jax.experimental import pallas as pl
from jax.experimental.pallas import tpu as pltpu
from jax.sharding import PartitionSpec as P

HALO = 32
PTS = 8
LANES = 128
ROWS = 16
MESH = pl.DeviceIdType.MESH


def taper(distance, half_width):
    relative = jnp.abs(distance) / half_width
    near_part = (
        ((-0.25 * relative + 0.5) * relative + 0.625) * relative - 5.0 / 3.0
    ) * relative * relative + 1.0
    bounded = jnp.maximum(relative, 1.0)
    far_part = (
        ((((relative / 12.0 - 0.5) * relative + 0.625) * relative + 5.0 / 3.0) * relative - 5.0)
        * relative
        + 4.0
        - 2.0 / (3.0 * bounded)
    )
    return jnp.where(relative <= 1.0, near_part, jnp.where(relative <= 2.0, far_part, 0.0))


def kernel(
    ncols, nchan, anom, jac, fc_h, fw_h, ow_h, cnt_s, rad, gram, *scratch
):
    members = anom.shape[1]
    tile = anom.shape[0]
    obs, chans = jac.shape[0], jac.shape[1]
    slots = obs * nchan
    width = chans // nchan
    packs = LANES // width
    group = ROWS // packs
    chunks = members // ROWS
    rows = members // nchan
    foot = fc_h.shape[0]
    total = tile * ncols
    ext = scratch[:chunks]
    (jbuf, stage, sbuf, rbuf, rstore, wf, cent, loc, gs, gacc, gsend, grecv,
     sem_loc, sem_jac, sem_hs, sem_hr, sem_fs, sem_fr, sem_ss, sem_rs, sem_own,
     sem_gs, sem_gr, fc_s, fw_s, fc_v, fw_v, ow_v, sem_in) = scratch[chunks:]

    col = lax.axis_index("cols")
    chan = lax.axis_index("chan")
    core = lax.rem(chan, 2)
    partner = chan + 1 - 2 * core
    step = 1 - 2 * core
    ahead = lax.rem(col + step + ncols, ncols)
    behind = lax.rem(col - step + ncols, ncols)
    first = chan * obs

    barrier = pltpu.get_barrier_semaphore()
    for where in (ahead, behind):
        pl.semaphore_signal(barrier, inc=1, device_id=(where, chan), device_id_type=MESH)
    for d in range(1, nchan):
        pl.semaphore_signal(
            barrier, inc=1, device_id=(col, lax.rem(chan + d, nchan)), device_id_type=MESH
        )

    inputs = []
    for i, (source, target) in enumerate(
        ((fc_h, fc_v), (fw_h, fw_v), (fc_h, fc_s), (fw_h, fw_s), (ow_h, ow_v))
    ):
        copy = pltpu.make_async_copy(source, target, sem_in.at[i])
        copy.start()
        inputs.append(copy)

    pl.semaphore_wait(barrier, nchan + 1)
    src_col = (tile - HALO) * (1 - core)
    dst_col = (tile + HALO) * core
    halos = []
    for k in range(chunks):
        copy = pltpu.make_async_remote_copy(
            src_ref=anom.at[pl.ds(src_col, HALO), pl.ds(k * ROWS, ROWS), :],
            dst_ref=ext[k].at[pl.ds(dst_col, HALO)],
            send_sem=sem_hs.at[k],
            recv_sem=sem_hr.at[k],
            device_id=(ahead, chan),
            device_id_type=MESH,
        )
        copy.start()
        halos.append(copy)

    locals_ = []
    for k in range(chunks):
        copy = pltpu.make_async_copy(
            anom.at[:, pl.ds(k * ROWS, ROWS), :], ext[k].at[pl.ds(HALO, tile)], sem_loc.at[k]
        )
        copy.start()
        locals_.append(copy)
        if k == 0:
            jcopy = pltpu.make_async_copy(jac, jbuf, sem_jac.at[0])
            jcopy.start()

    for copy in inputs:
        copy.wait()

    def offset_of(value):
        value = value - col * tile + HALO
        value = jnp.where(value < 0, value + total, value)
        return jnp.where(value >= total, value - total, value)

    gains = fw_v[...]
    offsets = (offset_of(fc_v[...]) - HALO).astype(jnp.float32)
    center = jnp.sum(gains * offsets, axis=0, keepdims=True) / jnp.sum(
        gains, axis=0, keepdims=True
    )
    cent[...] = jnp.transpose(jnp.broadcast_to(center, (LANES, slots)))
    mine = cent[pl.ds(pl.multiple_of(first, 8), obs), :]
    spacing = tile / PTS
    for p in range(PTS):
        loc[p] = taper(mine - (p + 0.5) * spacing, spacing) * (1.0 / (chans * slots))
    wf[...] = ow_v[...].astype(jnp.float32)

    lane = lax.broadcasted_iota(jnp.int32, (group, LANES), 1)
    live_count = cnt_s[0]
    jcopy.wait()

    forwards = []

    def pass_on(k):
        halos[k].wait_recv()
        copy = pltpu.make_async_remote_copy(
            src_ref=ext[k].at[pl.ds(dst_col, HALO)],
            dst_ref=ext[k].at[pl.ds(dst_col, HALO)],
            send_sem=sem_fs.at[k],
            recv_sem=sem_fr.at[k],
            device_id=(col, partner),
            device_id_type=MESH,
        )
        copy.start()
        forwards.append(copy)

    sends = []
    pass_on(0)
    for k in range(chunks):
        if k + 1 < chunks:
            pass_on(k + 1)
        locals_[k].wait()
        forwards[k].wait_recv()

        def one(n, carry, k=k):
            slot = first + n
            mixed = None
            for f in range(foot):
                at = jnp.minimum(offset_of(fc_s[f, slot]), tile + 2 * HALO - 1)
                at = jnp.maximum(at, 0)
                part = fw_s[f, slot] * ext[k][at].astype(jnp.float32)
                mixed = part if mixed is None else mixed + part
            live = jnp.where(slot < live_count, 1.0, 0.0).astype(jnp.float32)
            radiance = lax.dot_general(
                mixed.astype(jnp.bfloat16), jbuf[n], (((1,), (1,)), ((), ())),
                preferred_element_type=jnp.float32,
            ) * live
            rstore[n, k * ROWS:(k + 1) * ROWS, :] = radiance.astype(jnp.bfloat16)
            for q in range(nchan):
                start = q * width
                block, shift = start // LANES * LANES, start % LANES
                piece = None
                for h in range(packs):
                    part = radiance[h * group:(h + 1) * group, block:block + LANES]
                    turn = (h * width - shift) % LANES
                    if turn:
                        part = pltpu.roll(part, turn, 1)
                    piece = part if piece is None else jnp.where(lane < h * width, piece, part)
                stage[q, pl.ds(n, group, stride=obs), :] = piece
            return carry

        lax.fori_loop(0, obs, one, 0, unroll=4)
        for q in range(nchan):
            sbuf[k, q] = stage[q].astype(jnp.bfloat16).reshape(group, obs, LANES)
        place = pl.ds(pl.multiple_of(first, obs), obs)
        for d in range(1, nchan):
            to = lax.rem(chan + d, nchan)
            copy = pltpu.make_async_remote_copy(
                src_ref=sbuf.at[k, to],
                dst_ref=rbuf.at[k, :, place, :],
                send_sem=sem_ss.at[k, d],
                recv_sem=sem_rs.at[k, d],
                device_id=(col, to),
                device_id_type=MESH,
            )
            copy.start()
            sends.append((k, copy))
        own = pltpu.make_async_copy(sbuf.at[k, chan], rbuf.at[k, :, place, :], sem_own.at[k])
        own.start()
        sends.append((k, own))
        forwards[k].wait_send()
        halos[k].wait_send()

    def product(n, carry):
        values = rstore[n]
        weighted = (values.astype(jnp.float32) * wf[pl.ds(n, 1), :]).astype(jnp.bfloat16)
        gs[n] = lax.dot_general(
            weighted, values, (((1,), (1,)), ((), ())), preferred_element_type=jnp.float32
        )
        return carry

    lax.fori_loop(0, obs, product, 0, unroll=4)

    def point(p, carry):
        sums = [None, None]
        for n in range(obs):
            value = gs[n]
            for i in range(2):
                part = loc[2 * p + i, pl.ds(n, 1), :][:, :members] * value
                sums[i] = part if sums[i] is None else sums[i] + part
        for i in range(2):
            gacc[2 * p + i] = sums[i]
        return carry

    lax.fori_loop(0, PTS // 2, point, 0)
    for q in range(nchan):
        gsend[q] = gacc[:, q * rows:(q + 1) * rows, :].astype(jnp.bfloat16)
    gsends = []
    for d in range(1, nchan):
        to = lax.rem(chan + d, nchan)
        copy = pltpu.make_async_remote_copy(
            src_ref=gsend.at[to],
            dst_ref=grecv.at[d],
            send_sem=sem_gs.at[d],
            recv_sem=sem_gr.at[d],
            device_id=(col, to),
            device_id_type=MESH,
        )
        copy.start()
        gsends.append(copy)

    for k in range(chunks):
        for at, copy in sends:
            if at == k:
                copy.wait()

        def turn_one(j, carry, k=k):
            turned = jnp.transpose(rbuf[k, j].astype(jnp.float32)).astype(jnp.bfloat16)
            for h in range(packs):
                rad[k * ROWS + h * group + j] = turned[h * width:(h + 1) * width]
            return carry

        lax.fori_loop(0, group, turn_one, 0, unroll=2)

    result = gsend[chan].astype(jnp.float32)
    for d in range(1, nchan):
        gsends[d - 1].wait()
        result = result + grecv[d].astype(jnp.float32)
    gram[...] = result


def shards(ncols, nchan, anomaly, jacobian, foot_cols, foot_weight, obs_count, obs_weight):
    tile, members, levels = anomaly.shape
    obs, chans = jacobian.shape[:2]
    slots, foot = foot_cols.shape
    width = chans // nchan
    group = ROWS // (LANES // width)
    chunks = members // ROWS
    rows = members // nchan
    vmem = pl.BlockSpec(memory_space=pltpu.VMEM)
    hbm = pl.BlockSpec(memory_space=pltpu.HBM)
    dma = pltpu.SemaphoreType.DMA
    return pl.pallas_call(
        functools.partial(kernel, ncols, nchan),
        out_shape=(
            jax.ShapeDtypeStruct((members, width, slots), jnp.bfloat16),
            jax.ShapeDtypeStruct((PTS, rows, members), jnp.float32),
        ),
        in_specs=[*[hbm] * 5, pl.BlockSpec(memory_space=pltpu.SMEM)],
        out_specs=(vmem, vmem),
        scratch_shapes=[
            *[pltpu.VMEM((tile + 2 * HALO, ROWS, levels), jnp.bfloat16) for _ in range(chunks)],
            pltpu.VMEM((obs, chans, levels), jnp.bfloat16),
            pltpu.VMEM((nchan, group * obs, LANES), jnp.float32),
            pltpu.VMEM((chunks, nchan, group, obs, LANES), jnp.bfloat16),
            pltpu.VMEM((chunks, group, slots, LANES), jnp.bfloat16),
            pltpu.VMEM((obs, members, chans), jnp.bfloat16),
            pltpu.VMEM((obs, chans), jnp.float32),
            pltpu.VMEM((slots, LANES), jnp.float32),
            pltpu.VMEM((PTS, obs, LANES), jnp.float32),
            pltpu.VMEM((obs, members, members), jnp.float32),
            pltpu.VMEM((PTS, members, members), jnp.float32),
            pltpu.VMEM((nchan, PTS, rows, members), jnp.bfloat16),
            pltpu.VMEM((nchan, PTS, rows, members), jnp.bfloat16),
            dma((chunks,)),
            dma((1,)),
            dma((chunks,)),
            dma((chunks,)),
            dma((chunks,)),
            dma((chunks,)),
            dma((chunks, nchan)),
            dma((chunks, nchan)),
            dma((chunks,)),
            dma((nchan,)),
            dma((nchan,)),
            pltpu.SMEM((foot, slots), jnp.int32),
            pltpu.SMEM((foot, slots), jnp.float32),
            pltpu.VMEM((foot, slots), jnp.int32),
            pltpu.VMEM((foot, slots), jnp.float32),
            pltpu.VMEM((obs, chans), jnp.bfloat16),
            dma((5,)),
        ],
        compiler_params=pltpu.CompilerParams(
            collective_id=0, has_side_effects=True, vmem_limit_bytes=48 * 1024 * 1024
        ),
    )(
        *(
            pltpu.with_memory_space_constraint(x, pltpu.HBM)
            for x in (anomaly, jacobian, foot_cols.T, foot_weight.T, obs_weight.T)
        ),
        obs_count,
    )


def solution(mesh):
    return jax.shard_map(
        functools.partial(shards, mesh.shape["cols"], mesh.shape["chan"]),
        mesh=mesh,
        in_specs=(
            P("cols", None, None),
            P(("cols", "chan"), None, None),
            P("cols", None),
            P("cols", None),
            P("cols"),
            P(None, ("cols", "chan")),
        ),
        out_specs=(P(None, "chan", "cols"), P("cols", "chan", None)),
        check_vma=False,
    )
```

```python
import functools

import jax
import jax.numpy as jnp
from jax import lax
from jax.experimental import pallas as pl
from jax.experimental.pallas import tpu as pltpu
from jax.sharding import PartitionSpec as P

HALO = 32
PTS = 8
LANES = 128
ROWS = 8
MESH = pl.DeviceIdType.MESH


def taper(distance, half_width):
    relative = jnp.abs(distance) / half_width
    near_part = (
        ((-0.25 * relative + 0.5) * relative + 0.625) * relative - 5.0 / 3.0
    ) * relative * relative + 1.0
    bounded = jnp.maximum(relative, 1.0)
    far_part = (
        ((((relative / 12.0 - 0.5) * relative + 0.625) * relative + 5.0 / 3.0) * relative - 5.0)
        * relative
        + 4.0
        - 2.0 / (3.0 * bounded)
    )
    return jnp.where(relative <= 1.0, near_part, jnp.where(relative <= 2.0, far_part, 0.0))


def kernel(
    ncols, nchan, anom, jac, fc_h, fw_h, ow_h, cnt_s, rad, gram, *scratch
):
    members = anom.shape[1]
    tile = anom.shape[0]
    obs, chans = jac.shape[0], jac.shape[1]
    slots = obs * nchan
    width = chans // nchan
    packs = LANES // width
    group = ROWS // packs
    chunks = members // ROWS
    rows = members // nchan
    foot = fc_h.shape[0]
    total = tile * ncols
    ext = scratch[:chunks]
    (jbuf, stage, sbuf, rbuf, rstore, wf, cent, loc, gs, gacc, gsend, grecv,
     sem_loc, sem_jac, sem_hs, sem_hr, sem_fs, sem_fr, sem_ss, sem_rs, sem_own,
     sem_gs, sem_gr, fc_s, fw_s, fc_v, fw_v, ow_v, sem_in) = scratch[chunks:]

    col = lax.axis_index("cols")
    chan = lax.axis_index("chan")
    core = lax.rem(chan, 2)
    partner = chan + 1 - 2 * core
    step = 1 - 2 * core
    ahead = lax.rem(col + step + ncols, ncols)
    behind = lax.rem(col - step + ncols, ncols)
    first = chan * obs

    barrier = pltpu.get_barrier_semaphore()
    for where in (ahead, behind):
        pl.semaphore_signal(barrier, inc=1, device_id=(where, chan), device_id_type=MESH)
    for d in range(1, nchan):
        pl.semaphore_signal(
            barrier, inc=1, device_id=(col, lax.rem(chan + d, nchan)), device_id_type=MESH
        )

    inputs = []
    for i, (source, target) in enumerate(
        ((fc_h, fc_v), (fw_h, fw_v), (fc_h, fc_s), (fw_h, fw_s), (ow_h, ow_v))
    ):
        copy = pltpu.make_async_copy(source, target, sem_in.at[i])
        copy.start()
        inputs.append(copy)

    pl.semaphore_wait(barrier, nchan + 1)
    src_col = (tile - HALO) * (1 - core)
    dst_col = (tile + HALO) * core
    halos = []
    for k in range(chunks):
        copy = pltpu.make_async_remote_copy(
            src_ref=anom.at[pl.ds(src_col, HALO), pl.ds(k * ROWS, ROWS), :],
            dst_ref=ext[k].at[pl.ds(dst_col, HALO)],
            send_sem=sem_hs.at[k],
            recv_sem=sem_hr.at[k],
            device_id=(ahead, chan),
            device_id_type=MESH,
        )
        copy.start()
        halos.append(copy)

    locals_ = []
    for k in range(chunks):
        copy = pltpu.make_async_copy(
            anom.at[:, pl.ds(k * ROWS, ROWS), :], ext[k].at[pl.ds(HALO, tile)], sem_loc.at[k]
        )
        copy.start()
        locals_.append(copy)
        if k == 0:
            jcopy = pltpu.make_async_copy(jac, jbuf, sem_jac.at[0])
            jcopy.start()

    for copy in inputs:
        copy.wait()

    def offset_of(value):
        value = value - col * tile + HALO
        value = jnp.where(value < 0, value + total, value)
        return jnp.where(value >= total, value - total, value)

    gains = fw_v[...]
    offsets = (offset_of(fc_v[...]) - HALO).astype(jnp.float32)
    center = jnp.sum(gains * offsets, axis=0, keepdims=True) / jnp.sum(
        gains, axis=0, keepdims=True
    )
    cent[...] = jnp.transpose(jnp.broadcast_to(center, (LANES, slots)))
    mine = cent[pl.ds(pl.multiple_of(first, 8), obs), :]
    spacing = tile / PTS
    for p in range(PTS):
        loc[p] = taper(mine - (p + 0.5) * spacing, spacing) * (1.0 / (chans * slots))
    wf[...] = ow_v[...].astype(jnp.float32)

    lane = lax.broadcasted_iota(jnp.int32, (group, LANES), 1)
    live_count = cnt_s[0]
    jcopy.wait()

    forwards = []

    def pass_on(k):
        halos[k].wait_recv()
        copy = pltpu.make_async_remote_copy(
            src_ref=ext[k].at[pl.ds(dst_col, HALO)],
            dst_ref=ext[k].at[pl.ds(dst_col, HALO)],
            send_sem=sem_fs.at[k],
            recv_sem=sem_fr.at[k],
            device_id=(col, partner),
            device_id_type=MESH,
        )
        copy.start()
        forwards.append(copy)

    sends = []
    pass_on(0)
    for k in range(chunks):
        if k + 1 < chunks:
            pass_on(k + 1)
        locals_[k].wait()
        forwards[k].wait_recv()

        def one(n, carry, k=k):
            slot = first + n
            mixed = None
            for f in range(foot):
                at = jnp.minimum(offset_of(fc_s[f, slot]), tile + 2 * HALO - 1)
                at = jnp.maximum(at, 0)
                part = fw_s[f, slot] * ext[k][at].astype(jnp.float32)
                mixed = part if mixed is None else mixed + part
            live = jnp.where(slot < live_count, 1.0, 0.0).astype(jnp.float32)
            radiance = lax.dot_general(
                mixed.astype(jnp.bfloat16), jbuf[n], (((1,), (1,)), ((), ())),
                preferred_element_type=jnp.float32,
            ) * live
            rstore[n, k * ROWS:(k + 1) * ROWS, :] = radiance.astype(jnp.bfloat16)
            for q in range(nchan):
                start = q * width
                block, shift = start // LANES * LANES, start % LANES
                piece = None
                for h in range(packs):
                    part = radiance[h * group:(h + 1) * group, block:block + LANES]
                    turn = (h * width - shift) % LANES
                    if turn:
                        part = pltpu.roll(part, turn, 1)
                    piece = part if piece is None else jnp.where(lane < h * width, piece, part)
                stage[q, pl.ds(n, group, stride=obs), :] = piece
            return carry

        lax.fori_loop(0, obs, one, 0, unroll=16)
        for q in range(nchan):
            sbuf[k, q] = stage[q].astype(jnp.bfloat16).reshape(group, obs, LANES)
        place = pl.ds(pl.multiple_of(first, obs), obs)
        for d in range(1, nchan):
            to = lax.rem(chan + d, nchan)
            copy = pltpu.make_async_remote_copy(
                src_ref=sbuf.at[k, to],
                dst_ref=rbuf.at[k, :, place, :],
                send_sem=sem_ss.at[k, d],
                recv_sem=sem_rs.at[k, d],
                device_id=(col, to),
                device_id_type=MESH,
            )
            copy.start()
            sends.append((k, copy))
        own = pltpu.make_async_copy(sbuf.at[k, chan], rbuf.at[k, :, place, :], sem_own.at[k])
        own.start()
        sends.append((k, own))
        forwards[k].wait_send()
        halos[k].wait_send()

    def product(n, carry):
        values = rstore[n]
        weighted = (values.astype(jnp.float32) * wf[pl.ds(n, 1), :]).astype(jnp.bfloat16)
        gs[n] = lax.dot_general(
            weighted, values, (((1,), (1,)), ((), ())), preferred_element_type=jnp.float32
        )
        return carry

    lax.fori_loop(0, obs, product, 0, unroll=16)

    def point(p, carry):
        sums = [None, None]
        for n in range(obs):
            value = gs[n]
            for i in range(2):
                part = loc[2 * p + i, pl.ds(n, 1), :][:, :members] * value
                sums[i] = part if sums[i] is None else sums[i] + part
        for i in range(2):
            gacc[2 * p + i] = sums[i]
        return carry

    lax.fori_loop(0, PTS // 2, point, 0)
    for q in range(nchan):
        gsend[q] = gacc[:, q * rows:(q + 1) * rows, :].astype(jnp.bfloat16)
    gsends = []
    for d in range(1, nchan):
        to = lax.rem(chan + d, nchan)
        copy = pltpu.make_async_remote_copy(
            src_ref=gsend.at[to],
            dst_ref=grecv.at[d],
            send_sem=sem_gs.at[d],
            recv_sem=sem_gr.at[d],
            device_id=(col, to),
            device_id_type=MESH,
        )
        copy.start()
        gsends.append(copy)

    for k in range(chunks):
        for at, copy in sends:
            if at == k:
                copy.wait()

        def turn_one(j, carry, k=k):
            turned = jnp.transpose(rbuf[k, j].astype(jnp.float32)).astype(jnp.bfloat16)
            for h in range(packs):
                rad[k * ROWS + h * group + j] = turned[h * width:(h + 1) * width]
            return carry

        lax.fori_loop(0, group, turn_one, 0, unroll=2)

    result = gsend[chan].astype(jnp.float32)
    for d in range(1, nchan):
        gsends[d - 1].wait()
        result = result + grecv[d].astype(jnp.float32)
    gram[...] = result


def shards(ncols, nchan, anomaly, jacobian, foot_cols, foot_weight, obs_count, obs_weight):
    tile, members, levels = anomaly.shape
    obs, chans = jacobian.shape[:2]
    slots, foot = foot_cols.shape
    width = chans // nchan
    group = ROWS // (LANES // width)
    chunks = members // ROWS
    rows = members // nchan
    vmem = pl.BlockSpec(memory_space=pltpu.VMEM)
    hbm = pl.BlockSpec(memory_space=pltpu.HBM)
    dma = pltpu.SemaphoreType.DMA
    return pl.pallas_call(
        functools.partial(kernel, ncols, nchan),
        out_shape=(
            jax.ShapeDtypeStruct((members, width, slots), jnp.bfloat16),
            jax.ShapeDtypeStruct((PTS, rows, members), jnp.float32),
        ),
        in_specs=[*[hbm] * 5, pl.BlockSpec(memory_space=pltpu.SMEM)],
        out_specs=(vmem, vmem),
        scratch_shapes=[
            *[pltpu.VMEM((tile + 2 * HALO, ROWS, levels), jnp.bfloat16) for _ in range(chunks)],
            pltpu.VMEM((obs, chans, levels), jnp.bfloat16),
            pltpu.VMEM((nchan, group * obs, LANES), jnp.float32),
            pltpu.VMEM((chunks, nchan, group, obs, LANES), jnp.bfloat16),
            pltpu.VMEM((chunks, group, slots, LANES), jnp.bfloat16),
            pltpu.VMEM((obs, members, chans), jnp.bfloat16),
            pltpu.VMEM((obs, chans), jnp.float32),
            pltpu.VMEM((slots, LANES), jnp.float32),
            pltpu.VMEM((PTS, obs, LANES), jnp.float32),
            pltpu.VMEM((obs, members, members), jnp.float32),
            pltpu.VMEM((PTS, members, members), jnp.float32),
            pltpu.VMEM((nchan, PTS, rows, members), jnp.bfloat16),
            pltpu.VMEM((nchan, PTS, rows, members), jnp.bfloat16),
            dma((chunks,)),
            dma((1,)),
            dma((chunks,)),
            dma((chunks,)),
            dma((chunks,)),
            dma((chunks,)),
            dma((chunks, nchan)),
            dma((chunks, nchan)),
            dma((chunks,)),
            dma((nchan,)),
            dma((nchan,)),
            pltpu.SMEM((foot, slots), jnp.int32),
            pltpu.SMEM((foot, slots), jnp.float32),
            pltpu.VMEM((foot, slots), jnp.int32),
            pltpu.VMEM((foot, slots), jnp.float32),
            pltpu.VMEM((obs, chans), jnp.bfloat16),
            dma((5,)),
        ],
        compiler_params=pltpu.CompilerParams(
            collective_id=0, has_side_effects=True, vmem_limit_bytes=48 * 1024 * 1024
        ),
    )(
        *(
            pltpu.with_memory_space_constraint(x, pltpu.HBM)
            for x in (anomaly, jacobian, foot_cols.T, foot_weight.T, obs_weight.T)
        ),
        obs_count,
    )


def solution(mesh):
    return jax.shard_map(
        functools.partial(shards, mesh.shape["cols"], mesh.shape["chan"]),
        mesh=mesh,
        in_specs=(
            P("cols", None, None),
            P(("cols", "chan"), None, None),
            P("cols", None),
            P("cols", None),
            P("cols"),
            P(None, ("cols", "chan")),
        ),
        out_specs=(P(None, "chan", "cols"), P("cols", "chan", None)),
        check_vma=False,
    )
```
